32 devices in a mesh: tm: 8 (over z, y), order: 4 (over x, core).
Axes of the slice: x: 2, y: 2, z: 4, core: 2. Of those that a mesh axis runs over, the one named last changes fastest.
Arguments:
- longitude: float32 [32768], P('tm'), may hold values from -3.140625 to 3.140625
- node_index: int32 [32768], P('tm'), may hold values from 0 to 159
- weight: float32 [32768], P('tm'), may hold values from 0.5 to 2
- gradient: float32 [32768], P('tm'), may hold values from 2 to 6
- segment: int32 [32768], P('tm'), may hold values from 0 to 31, never falling along the last dimension, each value on 1 to 4096 neighbouring positions
- order_map: int32 [304], P('order'), may hold values from 0 to 303, each once
- legendre: bfloat16 [304, 160, 304], P('order'), may hold values from -0.0625 to 0.0625
- precond: float32 [19, 2, 304, 304], P(None, None, 'order'), may hold values from 0 to 1, as said below
- kaula_prior: float32 [2, 304, 304], P(None, 'order'), may hold values from 0.5 to 5
- start_iterate: float32 [2, 304, 304], P(None, 'order'), may hold values from -6 to 6
- direction: float32 [2, 304, 304], P(None, 'order'), may hold values from -6 to 6
Outputs:
- iterate: float32 [2, 304, 304], P(None, 'order')
- residual: float32 [2, 304, 304], P(None, 'order')
- new_direction: float32 [2, 304, 304], P(None, 'order')
The draws below stay inside these ranges and needn't reach their ends.
Inputs may be any that keep to these rules, and one draw needn't show every extreme that they name: `precond`: each block of 19 degrees is a symmetric positive definite matrix.
All inputs are finite; a program needn't handle non-finite values.
Results may differ from the reference program's by a relative error of at most 0.0003.
Values sent between devices are 32-bit elements; how exact they have to be, the bound alone decides.
No kernel may reach another device: no remote copies, remote signals or barrier semaphores. Data moves between devices by JAX's collectives and lax.ppermute only.
A program may use at most 128 MiB of HBM per device.

```python
import math
import jax
import jax.numpy as jnp
import numpy as np
from jax import lax

LMAX = 300
NDEG = 304
MSLOTS = 304
K = 160
DB = 19
ITERS = 2
R_DEV = 4096
ROWS = 32768
SEGS = 32
N_TM = 8


def draw_precond(key, part):
    key_off, key_diag, key_scale = jax.random.split(key, 3)
    blocks = NDEG // DB
    block_shape = (DB, 2, MSLOTS, blocks, DB)
    upper_part = jax.random.uniform(key_off, block_shape, jnp.float32, 0.01, 0.04)
    offdiag = 0.5 * (upper_part + jnp.transpose(upper_part, (4, 1, 2, 3, 0)))
    diagonal = jax.random.uniform(key_diag, block_shape, jnp.float32, 1.6, 2.4)
    on_diagonal = jnp.arange(DB)[:, None, None, None, None] == jnp.arange(DB)[None, None, None, None, :]
    block_core = jnp.where(on_diagonal, diagonal, offdiag)
    scale_low, scale_high = (0.3, 1.5)
    scales = jnp.exp(jax.random.uniform(key_scale, (2, MSLOTS, blocks, DB), jnp.float32, math.log(scale_low), math.log(scale_high)))
    column = jnp.transpose(scales, (3, 0, 1, 2))[..., None]
    row_scale = scales[None]
    return (0.1 * block_core * column * row_scale).reshape(DB, 2, MSLOTS, NDEG)


def set_ends(values, own_key, smallest, high):
    place = [jax.random.randint(jax.random.fold_in(own_key, axis), (), 0, length) for axis, length in enumerate(values.shape)]
    longest = values.shape.index(max(values.shape))
    beside = place[:longest] + [(place[longest] + 1) % values.shape[longest]] + place[longest + 1:]
    return values.at[tuple(place)].set(smallest).at[tuple(beside)].set(high)


def steps_of(own_key, shape, cuts, smallest, high):
    factor_of = 1.0
    for axis_at, blocks in cuts:
        steps = jax.random.uniform(jax.random.fold_in(jax.random.fold_in(own_key, 6), axis_at), (blocks,), jnp.float32, smallest / len(cuts), high / len(cuts))
        factor_of = factor_of * jnp.repeat(jnp.exp(steps), shape[axis_at] // blocks).reshape((-1,) + (1,) * (len(shape) - 1 - axis_at))
    return factor_of


def profile(count, total, reach, skew):
    portions = [(1 << 20) // math.isqrt(rank ** skew) + 1 for rank in range(2, count + 1)]
    spare, holding = total - reach - (count - 1), [1] * (count - 1)
    while spare > 0:
        movable = [i for i in range(count - 1) if holding[i] < reach]
        whole, budget = sum([portions[i] for i in movable]), spare
        for i in movable:
            addition = min(reach - holding[i], max(1, budget * portions[i] // whole), spare)
            holding[i] = holding[i] + addition
            spare = spare - addition
    return np.array([reach] + holding)


def uneven(own_key, amount, total, limit, skew):
    if amount == 2:
        one = jax.random.randint(own_key, (), max(1, total - limit), min(limit, total - 1) + 1)
        return jnp.stack([one, total - one])
    lengths = jnp.asarray(profile(amount, total, limit, skew), jnp.int32)
    pairs = (amount - 1) // 2
    giver, sink = lengths[1:1 + 2 * pairs:2], lengths[2:2 + 2 * pairs:2]
    room = jnp.minimum(giver - 1, limit - sink)
    passed = jax.random.randint(jax.random.fold_in(own_key, 1), (pairs,), 0, 1 << 20) % (room + 1)
    lengths = lengths.at[1:1 + 2 * pairs:2].set(giver - passed).at[2:2 + 2 * pairs:2].set(sink + passed)
    return lengths[jax.random.permutation(jax.random.fold_in(own_key, 2), amount)]


def bell_draw(rng, extent, spread, most, shards=(), kind=jnp.bfloat16):
    loudness = steps_of(rng, extent, shards, -0.22, 0.18) if shards else 1.0
    values = jax.random.normal(rng, extent, jnp.float32) * spread * loudness
    return jnp.minimum(jnp.maximum(values, -most), most).astype(kind)


def setup_inputs(seed: int = 0) -> dict:
    key_list = jax.random.split(jax.random.key(seed), 12)
    return {
        "longitude": jnp.clip(jax.random.uniform(key_list[0], (ROWS,), jnp.float32, -3.140625, 3.140625), -3.140625, 3.140625),
        "node_index": set_ends(jax.random.randint(key_list[1], (ROWS,), 0, K), jax.random.fold_in(key_list[1], 1), 0, K - 1).astype(jnp.int32),
        "weight": jnp.clip(jnp.exp(math.log(2.0) - 1.3862944 * jax.random.uniform(key_list[2], (ROWS,), jnp.float32) ** steps_of(key_list[2], (ROWS,), ((0, 8),), -0.2, 0.2)), 0.5, 2.0),
        "gradient": jnp.clip(2.0 + 4.0 * jax.random.uniform(key_list[3], (ROWS,), jnp.float32) ** steps_of(key_list[3], (ROWS,), ((0, 8),), -0.2, 0.2), 2.0, 6.0),
        "segment": jnp.searchsorted(jnp.cumsum(uneven(key_list[4], SEGS, ROWS, R_DEV, 0)), jnp.arange(ROWS), side="right").astype(jnp.int32),
        "order_map": jax.random.permutation(key_list[5], MSLOTS).astype(jnp.int32),
        "legendre": bell_draw(key_list[6], (MSLOTS, K, NDEG), (ROWS // 4) ** -0.5, 0.0625, ((0, 4),)),
        "precond": draw_precond(jax.random.fold_in(key_list[11], 71), 0),
        "kaula_prior": jnp.clip(jnp.exp(math.log(5.0) - 2.3025851 * jax.random.uniform(key_list[8], (2, MSLOTS, NDEG), jnp.float32) ** steps_of(key_list[8], (2, MSLOTS, NDEG), ((1, 4),), -0.2, 0.2)), 0.5, 5.0),
        "start_iterate": bell_draw(key_list[9], (2, MSLOTS, NDEG), 1.0, 6.0, ((1, 4),), jnp.float32),
        "direction": bell_draw(key_list[10], (2, MSLOTS, NDEG), 1.0, 6.0, ((1, 4),), jnp.float32),
    }


def valid_mask_of(order_map, degrees):
    order_ids = order_map[None, :, None]
    degree_ids = jnp.arange(degrees, dtype=jnp.int32)[None, None, :]
    part_ids = jnp.arange(2, dtype=jnp.int32)[:, None, None]
    keep = (degree_ids <= LMAX) & (degree_ids >= jnp.maximum(order_ids, 2)) & ((part_ids == 0) | (order_ids >= 1))
    return keep.astype(jnp.float32)


def make_phase(longitude, order_map):
    angle = longitude[:, None] * order_map.astype(jnp.float32)[None, :]
    return jnp.concatenate([jnp.cos(angle), jnp.sin(angle)], axis=1)


def node_select(node_index, node_count):
    return (jnp.arange(node_count, dtype=jnp.int32)[:, None] == node_index[None, :]).astype(jnp.float32)


def forward_all(vector, legendre, longitude, node_index, order_map):
    slot_count, node_count = legendre.shape[0], legendre.shape[1]
    nodal = jnp.einsum("mkn,cmn->kcm", legendre.astype(jnp.float32), vector, precision=lax.Precision.HIGHEST).reshape(node_count, 2 * slot_count)

    def block_rows(pieces):
        block_lon, block_nodes = pieces
        selector = node_select(block_nodes, node_count)
        row_terms = lax.dot_general(selector, nodal, (((0,), (0,)), ((), ())), precision=lax.Precision.HIGHEST)
        return jnp.sum(row_terms * make_phase(block_lon, order_map), axis=1)

    return lax.map(block_rows, (longitude.reshape(N_TM, R_DEV), node_index.reshape(N_TM, R_DEV))).reshape(-1)


def backward_all(weighted, legendre, longitude, node_index, order_map):
    slot_count, node_count = legendre.shape[0], legendre.shape[1]

    def accumulate(carry, pieces):
        block_lon, block_nodes, block_values = pieces
        selector = node_select(block_nodes, node_count)
        terms = make_phase(block_lon, order_map) * block_values[:, None]
        return carry + jnp.dot(selector, terms, precision=lax.Precision.HIGHEST), None

    start_sum = jnp.zeros((node_count, 2 * slot_count), jnp.float32)
    node_terms, _ = lax.scan(accumulate, start_sum, (longitude.reshape(N_TM, R_DEV), node_index.reshape(N_TM, R_DEV), weighted.reshape(N_TM, R_DEV)))
    node_terms = node_terms.reshape(node_count, 2, slot_count)
    return jnp.einsum("mkn,kcm->cmn", legendre.astype(jnp.float32), node_terms, precision=lax.Precision.HIGHEST)


def center_all(values, weight, segment):
    weight_sums = jax.ops.segment_sum(weight, segment, num_segments=SEGS)
    value_sums = jax.ops.segment_sum(weight * values, segment, num_segments=SEGS)
    means = value_sums / weight_sums
    return weight * (values - jnp.take(means, segment))


def precondition(blocks, vector):
    flat = vector.reshape(-1)
    block_count = flat.shape[0] // DB
    shaped = blocks.reshape(DB, block_count, DB)
    result = jnp.einsum("jbi,bj->bi", shaped, flat.reshape(block_count, DB), precision=lax.Precision.HIGHEST)
    return result.reshape(vector.shape)


def reference(longitude, node_index, weight, gradient, segment, order_map, legendre, precond, kaula_prior, start_iterate, direction):
    degrees = legendre.shape[2]
    valid_mask = valid_mask_of(order_map, degrees)
    iterate = start_iterate * valid_mask
    new_direction = direction * valid_mask
    predicted = forward_all(iterate, legendre, longitude, node_index, order_map)
    misfit = center_all(gradient - predicted, weight, segment)
    residual = valid_mask * (backward_all(misfit, legendre, longitude, node_index, order_map) - kaula_prior * iterate)
    for iteration in range(ITERS):
        predicted = forward_all(new_direction, legendre, longitude, node_index, order_map)
        centered = center_all(predicted, weight, segment)
        image = valid_mask * (backward_all(centered, legendre, longitude, node_index, order_map) + kaula_prior * new_direction)
        residual_dot = jnp.sum(residual * new_direction)
        curvature = jnp.sum(new_direction * image)
        step_size = residual_dot / curvature
        iterate = iterate + step_size * new_direction
        residual = residual - step_size * image
        smoothed = valid_mask * precondition(precond, residual)
        conj_dot = jnp.sum(smoothed * image)
        new_direction = smoothed - (conj_dot / curvature) * new_direction
    return iterate, residual, new_direction
```

```python
import functools

import jax
import jax.numpy as jnp
from jax import lax
from jax.experimental import pallas as pl
from jax.experimental.pallas import tpu as pltpu
from jax.sharding import PartitionSpec as P

LMAX = 300
DB = 19
SUB = 8
F32 = jnp.float32
BF16 = jnp.bfloat16
NT = (((1,), (1,)), ((), ()))
NN = (((1,), (0,)), ((), ()))
VMEM = pl.BlockSpec(memory_space=pltpu.VMEM)
ANY = pl.BlockSpec(memory_space=pl.ANY)
LIMIT = 60 * 1024 * 1024


def mm(a, b, dims=NN):
    return lax.dot_general(a, b, dims, preferred_element_type=F32)


def split2(x):
    hi = x.astype(BF16)
    return hi, (x - hi.astype(F32)).astype(BF16)


def split3(x):
    hi = x.astype(BF16)
    rest = x - hi.astype(F32)
    mid = rest.astype(BF16)
    return hi, mid, (rest - mid.astype(F32)).astype(BF16)


def pad_to(x, rows):
    if x.shape[0] == rows:
        return x
    return jnp.concatenate([x, jnp.zeros((rows - x.shape[0],) + x.shape[1:], x.dtype)], axis=0)


def sincos(angle):
    quadrant = jnp.floor(angle * 0.6366197723675814 + 0.5)
    r = angle - quadrant * 1.5703125
    r = r - quadrant * 4.8351287841796875e-4
    r = r - quadrant * 3.1385570764541626e-7
    r = r - quadrant * 6.077100506506192e-11
    q = quadrant.astype(jnp.int32)
    z = r * r
    s = ((-1.9515295891e-4 * z + 8.3321608736e-3) * z - 1.6666654611e-1) * z * r + r
    c = ((2.443315711809948e-5 * z - 1.388731625493765e-3) * z + 4.166664568298827e-2) * z * z
    c = c - 0.5 * z + 1.0
    swap = (q & 1) == 1
    cos = jnp.where(swap, s, c)
    sin = jnp.where(swap, c, s)
    cos = jnp.where(((q + 1) & 2) == 2, -cos, cos)
    sin = jnp.where((q & 2) == 2, -sin, sin)
    return cos, sin


def one_hot(count, ids):
    rows = lax.broadcasted_iota(jnp.int32, (count, ids.shape[1]), 0)
    return jnp.where(rows == ids, 1.0, 0.0).astype(BF16)


def mask_of(order, part, degrees):
    n = lax.broadcasted_iota(jnp.int32, (order.shape[0], degrees), 1)
    keep = (n <= LMAX) & (n >= jnp.maximum(order, 2))
    if part == 1:
        keep = keep & (order >= 1)
    return keep


def chunks_of(rows):
    size = 512 if rows % 512 == 0 else rows
    return [(i, size) for i in range(0, rows, size)]


def leg_copies(leg_hbm, leg, sems):
    slots = leg.shape[0]
    out = []
    for g in range(-(-slots // SUB)):
        part = pl.ds(g * SUB, min(SUB, slots - g * SUB))
        out.append(pltpu.make_async_copy(leg_hbm.at[part], leg.at[part], sems.at[g]))
    return out


def order_group(leg, copies, g, x, dims):
    if copies is not None:
        copies[g].wait()
    hi, lo = split2(x)
    x2 = jnp.concatenate([hi, lo], axis=0)
    sub = lax.broadcasted_iota(jnp.int32, x2.shape, 0) % SUB
    total = None
    for i in range(min(SUB, leg.shape[0] - g * SUB)):
        term = mm(jnp.where(sub == i, x2, jnp.zeros_like(x2)), leg[g * SUB + i], dims)
        total = term if total is None else total + term
    return total[: x.shape[0]] + total[x.shape[0] :]


def nodal_of(leg, copies, vectors, nodal_ref, pad):
    groups = -(-leg.shape[0] // SUB)
    for g in range(groups):
        x = jnp.concatenate([f(g) for v in vectors for f in v], axis=0)
        y = order_group(leg, copies, g, x, NT)
        for v in range(len(vectors)):
            for c in range(2):
                at = (2 * v + c) * SUB
                row = v * 2 * pad + c * pad + g * SUB
                nodal_ref[row : row + SUB, :] = y[at : at + SUB]


def rows_of(nodal_ref, phase_ref, node_ref, out_ref, count):
    nodes = nodal_ref.shape[1]
    wide = nodal_ref.shape[0] // count
    hi, lo = split2(nodal_ref[...])
    for at, size in chunks_of(node_ref.shape[1]):
        sel = one_hot(nodes, node_ref[:, at : at + size])
        terms = mm(hi, sel) + mm(lo, sel)
        ph = phase_ref[:, at : at + size]
        for v in range(count):
            part = terms[v * wide : (v + 1) * wide] * ph
            out_ref[v : v + 1, at : at + size] = jnp.sum(part, axis=0, keepdims=True)


def gather_nodes(u_list, phase_ref, node_ref, nodes):
    totals = [None] * len(u_list)
    for at, size in chunks_of(node_ref.shape[1]):
        sel = one_hot(nodes, node_ref[:, at : at + size])
        ph = phase_ref[:, at : at + size]
        for v, u in enumerate(u_list):
            hi, lo = split2(ph * u[:, at : at + size])
            term = mm(hi, sel, NT) + mm(lo, sel, NT)
            totals[v] = term if totals[v] is None else totals[v] + term
    return totals


def phase_kernel(lon_ref, node_ref, weight_ref, seg_ref, order_ref, phase_ref, edge_ref):
    rows = lon_ref.shape[1]
    pad = order_ref.shape[0]
    nodes = edge_ref.shape[2]
    order = order_ref[...].astype(F32)
    for at, size in chunks_of(rows):
        cos, sin = sincos(lon_ref[:, at : at + size] * order)
        phase_ref[0:pad, at : at + size] = cos
        phase_ref[pad : 2 * pad, at : at + size] = sin
    seg = seg_ref[...]
    first = jnp.min(seg, axis=1, keepdims=True)
    last = jnp.max(seg, axis=1, keepdims=True)
    w = weight_ref[...]
    parts = [jnp.where(seg == last, w, 0.0), jnp.where(seg == first, w, 0.0)]
    totals = gather_nodes(parts, phase_ref, node_ref, nodes)
    column = lax.broadcasted_iota(jnp.int32, (SUB, nodes), 1)
    for e, (ident, part) in enumerate(zip((last, first), parts)):
        edge_ref[e, 0 : 2 * pad, :] = totals[e]
        amount = jnp.sum(part, axis=1, keepdims=True)
        stats = jnp.where(column == 0, amount, ident.astype(F32) + 1.0)
        edge_ref[e, 2 * pad :, :] = stats


def forward_kernel(phase_ref, node_ref, order_ref, x_ref, d_ref, leg_hbm, out_ref, leg, nodal, sems):
    copies = leg_copies(leg_hbm, leg, sems)
    for copy in copies:
        copy.start()
    pad = order_ref.shape[0]
    slots, degrees = x_ref.shape[1], x_ref.shape[2]

    def reader(ref, c):
        def read(g):
            top = min(SUB, slots - g * SUB)
            value = ref[c, g * SUB : g * SUB + top, :]
            keep = mask_of(order_ref[g * SUB : g * SUB + top, :], c, degrees)
            return pad_to(jnp.where(keep, value, 0.0), SUB)

        return read

    vectors = [[reader(ref, c) for c in range(2)] for ref in (x_ref, d_ref)]
    nodal_of(leg, copies, vectors, nodal, pad)
    rows_of(nodal, phase_ref, node_ref, out_ref, 2)


def centered(e_list, weight, seg, prev_row, next_row, segments):
    rows = seg.shape[1]
    ids = lax.broadcasted_iota(jnp.int32, (segments, rows), 0)
    sel = jnp.where(ids == seg, 1.0, 0.0).astype(BF16)
    stack = [weight] + [weight * e for e in e_list]
    pieces = [p for s in stack for p in split3(s)]
    fill = -len(pieces) % 16
    pieces = pieces + [jnp.zeros((fill, rows), BF16)] * (fill > 0)
    sums = mm(jnp.concatenate(pieces, axis=0), sel, NT)
    sums = [sums[3 * i : 3 * i + 1] + sums[3 * i + 1 : 3 * i + 2] + sums[3 * i + 2 : 3 * i + 3] for i in range(len(stack))]
    first = jnp.min(seg, axis=1, keepdims=True)
    last = jnp.max(seg, axis=1, keepdims=True)
    lane = lax.broadcasted_iota(jnp.int32, (1, segments), 1)
    at_first, at_last = lane == first, lane == last
    join_prev = jnp.where(prev_row[:, 1:2] == first.astype(F32) + 1.0, 1.0, 0.0)
    join_next = jnp.where(next_row[:, 1:2] == last.astype(F32) + 1.0, 1.0, 0.0)
    whole = sums[0]
    whole = whole + jnp.where(at_first, join_prev * prev_row[:, 0:1], 0.0)
    whole = whole + jnp.where(at_last, join_next * next_row[:, 0:1], 0.0)
    whole = jnp.where(whole > 0.0, whole, 1.0)
    means = [s / whole for s in sums[1:]]
    pieces = [p for m in means for p in split3(m)]
    fill = -len(pieces) % 16
    pieces = pieces + [jnp.zeros((fill, segments), BF16)]
    spread = mm(jnp.concatenate(pieces, axis=0), sel)
    out = []
    for i, m in enumerate(means):
        mean = spread[3 * i : 3 * i + 1] + spread[3 * i + 1 : 3 * i + 2] + spread[3 * i + 2 : 3 * i + 3]
        to_prev = join_prev * jnp.sum(jnp.where(at_first, m, 0.0), axis=1, keepdims=True)
        to_next = join_next * jnp.sum(jnp.where(at_last, m, 0.0), axis=1, keepdims=True)
        out.append((weight * (e_list[i] - mean), to_prev, to_next))
    return out


def center_and_gather(e_list, weight_ref, seg_ref, phase_ref, node_ref, prev_ref, next_ref, out_ref, segments):
    wide, nodes = out_ref.shape[1], out_ref.shape[2]
    prev_row, next_row = (r[wide : wide + 1, :] for r in (prev_ref, next_ref))
    done = centered(e_list, weight_ref[...], seg_ref[...], prev_row, next_row, segments)
    totals = gather_nodes([u for u, _, _ in done], phase_ref, node_ref, nodes)
    for v, (_, to_prev, to_next) in enumerate(done):
        out_ref[v, :, :] = totals[v] - to_prev * prev_ref[0:wide, :] - to_next * next_ref[0:wide, :]


def back_first_kernel(segments, p_ref, grad_ref, weight_ref, seg_ref, phase_ref, node_ref, prev_ref, next_ref, out_ref):
    e_list = [grad_ref[...] - p_ref[0:1, :], p_ref[1:2, :]]
    center_and_gather(e_list, weight_ref, seg_ref, phase_ref, node_ref, prev_ref, next_ref, out_ref, segments)


def scalars_of(row):
    return [row[:, i : i + 1] for i in range(4)]


def back_next_kernel(segments, p_ref, before_ref, weight_ref, seg_ref, phase_ref, node_ref, prev_ref, next_ref, out_ref):
    rows = seg_ref.shape[1]
    step, beta = steps_of(p_ref[0:1, rows : rows + 4])
    e = p_ref[0:1, 0:rows] - step * p_ref[1:2, 0:rows] - beta * before_ref[1:2, :]
    center_and_gather([e], weight_ref, seg_ref, phase_ref, node_ref, prev_ref, next_ref, out_ref, segments)


def steps_of(row):
    residual_dot, curvature, first, second = scalars_of(row)
    step = residual_dot / curvature
    return step, (first - step * second) / curvature


def lifted(leg, copies, gathered_ref, count, pad, store):
    groups = -(-leg.shape[0] // SUB)
    for g in range(groups):
        x = jnp.concatenate(
            [gathered_ref[v, c * pad + g * SUB : c * pad + (g + 1) * SUB, :] for v in range(count) for c in range(2)],
            axis=0,
        )
        y = order_group(leg, copies, g, x, NN)
        for v in range(count):
            for c in range(2):
                at = (2 * v + c) * SUB
                store(v, c, g, y[at : at + SUB])


def precondition(pre, start_row, vectors_ref, out_ref, count, pad):
    degrees = vectors_ref.shape[1]
    hi, lo = split2(vectors_ref[...])
    slots = pre.shape[2]
    source = lax.broadcasted_iota(jnp.int32, (degrees, degrees), 0) - start_row
    out_ref[...] = jnp.zeros_like(out_ref)
    for l in range(DB):
        spread = jnp.where(source == l, 1.0, 0.0).astype(BF16)
        wide = mm(hi, spread) + mm(lo, spread)
        for v in range(count):
            for c in range(2):
                at = (2 * v + c) * pad
                out_ref[at : at + slots, :] += pre[l, c] * wide[at : at + slots]


def dot_sum(pairs):
    total = None
    for a, b in pairs:
        term = jnp.sum(jnp.sum(a * b, axis=1, keepdims=True), axis=0, keepdims=True)
        total = term if total is None else total + term
    return total


def scalar_row(values, width):
    lane = lax.broadcasted_iota(jnp.int32, (1, width), 1)
    row = jnp.zeros((1, width), F32)
    for i, value in enumerate(values):
        row = jnp.where(lane == i, value, row)
    return row


def middle_kernel(
    gathered_ref, phase_ref, node_ref, order_ref, start_ref, kaula_ref, x_ref, d_ref, leg_hbm, pre_hbm,
    out_ref, r_ref, q_ref, pr_ref, pq_ref,
    leg, pre, nodal, vec, smooth, sems, pre_sem,
):
    copies = leg_copies(leg_hbm, leg, sems)
    for copy in copies:
        copy.start()
    pre_copy = pltpu.make_async_copy(pre_hbm, pre, pre_sem)
    pre_copy.start()
    pad = order_ref.shape[0]
    slots, degrees = x_ref.shape[1], x_ref.shape[2]
    rows = node_ref.shape[1]

    def store(v, c, g, y):
        at = (2 * v + c) * pad + g * SUB
        top = min(SUB, slots - g * SUB)
        part = slice(g * SUB, g * SUB + top)
        keep = mask_of(order_ref[part, :], c, degrees)
        k = kaula_ref[c, part, :]
        value = y[:top] - k * x_ref[c, part, :] if v == 0 else y[:top] + k * d_ref[c, part, :]
        vec[at : at + SUB, :] = pad_to(jnp.where(keep, value, 0.0), SUB)

    lifted(leg, copies, gathered_ref, 2, pad, store)
    pre_copy.wait()
    precondition(pre, start_ref[...], vec, smooth, 2, pad)
    dots = [[], [], [], []]
    for c in range(2):
        keep = mask_of(order_ref[0:slots, :], c, degrees)
        a, b = c * pad, (2 + c) * pad
        r, q = vec[a : a + slots, :], vec[b : b + slots, :]
        pr = jnp.where(keep, smooth[a : a + slots, :], 0.0)
        pq = jnp.where(keep, smooth[b : b + slots, :], 0.0)
        d = jnp.where(keep, d_ref[c], 0.0)
        smooth[a : a + slots, :] = pr
        smooth[b : b + slots, :] = pq
        r_ref[c], q_ref[c], pr_ref[c], pq_ref[c] = r, q, pr, pq
        for i, pair in enumerate(((r, d), (d, q), (pr, q), (pq, q))):
            dots[i].append(pair)
    out_ref[0:1, rows:] = scalar_row([dot_sum(p) for p in dots], out_ref.shape[1] - rows)
    out_ref[1:2, rows:] = jnp.zeros((1, out_ref.shape[1] - rows), F32)

    def reader(v, c):
        return lambda g: smooth[(2 * v + c) * pad + g * SUB : (2 * v + c) * pad + (g + 1) * SUB, :]

    nodal_of(leg, None, [[reader(v, c) for c in range(2)] for v in range(2)], nodal, pad)
    rows_of(nodal, phase_ref, node_ref, out_ref, 2)


def last_kernel(
    gathered_ref, row_ref, order_ref, start_ref, kaula_ref, x_ref, d_ref, r_ref, q_ref, pr_ref, pq_ref, leg_hbm, pre_hbm,
    dots_ref, q1_ref, pq1_ref, x1_ref, d1_ref, r1_ref, pr1_ref,
    leg, pre, vec, smooth, sems, pre_sem,
):
    copies = leg_copies(leg_hbm, leg, sems)
    for copy in copies:
        copy.start()
    pre_copy = pltpu.make_async_copy(pre_hbm, pre, pre_sem)
    pre_copy.start()
    pad = order_ref.shape[0]
    slots, degrees = x_ref.shape[1], x_ref.shape[2]
    step, beta = steps_of(row_ref[0:1, 0:4])
    for c in range(2):
        keep = mask_of(order_ref[0:slots, :], c, degrees)
        d = jnp.where(keep, d_ref[c], 0.0)
        pr1 = pr_ref[c] - step * pq_ref[c]
        x1_ref[c] = jnp.where(keep, x_ref[c], 0.0) + step * d
        r1_ref[c] = r_ref[c] - step * q_ref[c]
        pr1_ref[c] = pr1
        d1_ref[c] = pr1 - beta * d

    def store(v, c, g, y):
        at = c * pad + g * SUB
        top = min(SUB, slots - g * SUB)
        part = slice(g * SUB, g * SUB + top)
        keep = mask_of(order_ref[part, :], c, degrees)
        value = y[:top] + kaula_ref[c, part, :] * d1_ref[c, part, :]
        vec[at : at + SUB, :] = pad_to(jnp.where(keep, value, 0.0), SUB)

    lifted(leg, copies, gathered_ref, 1, pad, store)
    pre_copy.wait()
    precondition(pre, start_ref[...], vec, smooth, 1, pad)
    dots = [[], [], [], []]
    for c in range(2):
        keep = mask_of(order_ref[0:slots, :], c, degrees)
        q = vec[c * pad : c * pad + slots, :]
        pq = jnp.where(keep, smooth[c * pad : c * pad + slots, :], 0.0)
        q1_ref[c], pq1_ref[c] = q, pq
        d = d1_ref[c]
        for i, pair in enumerate(((r1_ref[c], d), (d, q), (pr1_ref[c], q), (pq, q))):
            dots[i].append(pair)
    dots_ref[...] = scalar_row([dot_sum(p) for p in dots], dots_ref.shape[1])


def butterfly(x, axis):
    size = lax.axis_size(axis)
    step = 1
    while step < size:
        x = x + lax.ppermute(x, axis, [(i, i ^ step) for i in range(size)])
        step *= 2
    return x


def call(kernel, outs, scratch, n_in, any_in=()):
    specs = [ANY if i in any_in else VMEM for i in range(n_in)]
    return pl.pallas_call(
        kernel,
        out_shape=[jax.ShapeDtypeStruct(s, F32) for s in outs],
        in_specs=specs,
        out_specs=[VMEM for _ in outs],
        scratch_shapes=scratch,
        compiler_params=pltpu.CompilerParams(vmem_limit_bytes=LIMIT),
    )


def shards(longitude, node_index, weight, gradient, segment, order_map, legendre, precond, kaula, start, direction):
    rows = longitude.shape[0]
    slots, nodes, degrees = legendre.shape
    pad = -(-slots // SUB) * SUB
    wide = 2 * pad
    segments = lax.axis_size("tm") * lax.axis_size("order")
    line = lambda v: v.reshape(1, rows)
    lon, node, w, grad, seg = (line(v) for v in (longitude, node_index, weight, gradient, segment))
    order = pad_to(order_map, pad).reshape(pad, 1)
    starts = ((jnp.arange(degrees, dtype=jnp.int32) // DB) * DB).reshape(1, degrees)
    coef = (2, slots, degrees)
    groups = -(-slots // SUB)
    leg_scratch = [pltpu.VMEM(legendre.shape, BF16)]
    leg_sems = pltpu.SemaphoreType.DMA((groups,))

    phase, edges = call(phase_kernel, [(wide, rows), (2, wide + SUB, nodes)], [], 5)(lon, node, w, seg, order)
    size = lax.axis_size("tm")
    up = [(i, i + 1) for i in range(size - 1)]
    prev_edge = lax.ppermute(edges[0], "tm", up)
    next_edge = lax.ppermute(edges[1], "tm", [(b, a) for a, b in up])

    (part,) = call(
        forward_kernel, [(2, rows)], leg_scratch + [pltpu.VMEM((2 * wide, nodes), F32), leg_sems], 6, (5,)
    )(phase, node, order, start, direction, legendre)
    first_rows = butterfly(part, "order")
    (part,) = call(functools.partial(back_first_kernel, segments), [(2, wide, nodes)], [], 8)(
        first_rows, grad, w, seg, phase, node, prev_edge, next_edge
    )
    gathered = butterfly(part, "tm")
    coef_scratch = leg_scratch + [pltpu.VMEM(precond.shape, F32)]
    part, r0, q0, pr0, pq0 = call(
        middle_kernel,
        [(2, rows + 128)] + [coef] * 4,
        coef_scratch
        + [pltpu.VMEM((2 * wide, nodes), F32)]
        + [pltpu.VMEM((2 * wide, degrees), F32)] * 2
        + [leg_sems, pltpu.SemaphoreType.DMA(())],
        10,
        (8, 9),
    )(gathered, phase, node, order, starts, kaula, start, direction, legendre, precond)
    next_rows = butterfly(part, "order")
    (part,) = call(functools.partial(back_next_kernel, segments), [(1, wide, nodes)], [], 8)(
        next_rows, first_rows, w, seg, phase, node, prev_edge, next_edge
    )
    gathered = butterfly(part, "tm")
    row = lax.slice(next_rows, (0, rows), (1, rows + 128))
    dots, q1, pq1, x1, d1, r1, pr1 = call(
        last_kernel,
        [(1, 128)] + [coef] * 6,
        coef_scratch + [pltpu.VMEM((wide, degrees), F32)] * 2 + [leg_sems, pltpu.SemaphoreType.DMA(())],
        13,
        (11, 12),
    )(gathered, row, order, starts, kaula, start, direction, r0, q0, pr0, pq0, legendre, precond)
    dots = butterfly(dots, "order")
    step, beta = (s[0, 0] for s in steps_of(dots))
    return x1 + step * d1, r1 - step * q1, pr1 - step * pq1 - beta * d1


def solution(mesh):
    coef = P(None, "order", None)
    placed = (P("tm"),) * 5 + (P("order"), P("order", None, None), P(None, None, "order", None), coef, coef, coef)
    return jax.shard_map(shards, mesh=mesh, in_specs=placed, out_specs=(coef, coef, coef), check_vma=False)
```

```python
import functools

import jax
import jax.numpy as jnp
from jax import lax
from jax.experimental import pallas as pl
from jax.experimental.pallas import tpu as pltpu
from jax.sharding import PartitionSpec as P

LMAX = 300
DB = 19
SUB = 8
HALF = 4
LANES = 128
LON, NODE, WEIGHT, SEG, GRAD, ORDER = range(6)
F32 = jnp.float32
BF16 = jnp.bfloat16
NT = (((1,), (1,)), ((), ()))
NN = (((1,), (0,)), ((), ()))
VMEM = pl.BlockSpec(memory_space=pltpu.VMEM)
HBM = pl.BlockSpec(memory_space=pltpu.HBM)
LIMIT = 28 * 1024 * 1024


def mm(a, b, dims=NN):
    return lax.dot_general(a, b, dims, preferred_element_type=F32)


def split2(x):
    hi = x.astype(BF16)
    return hi, (x - hi.astype(F32)).astype(BF16)


def split3(x):
    hi = x.astype(BF16)
    rest = x - hi.astype(F32)
    mid = rest.astype(BF16)
    return hi, mid, (rest - mid.astype(F32)).astype(BF16)


def sincos(angle):
    quadrant = jnp.floor(angle * 0.6366197723675814 + 0.5)
    r = angle - quadrant * 1.5703125
    r = r - quadrant * 4.8351287841796875e-4
    r = r - quadrant * 3.1385570764541626e-7
    r = r - quadrant * 6.077100506506192e-11
    q = quadrant.astype(jnp.int32)
    z = r * r
    s = ((-1.9515295891e-4 * z + 8.3321608736e-3) * z - 1.6666654611e-1) * z * r + r
    c = ((2.443315711809948e-5 * z - 1.388731625493765e-3) * z + 4.166664568298827e-2) * z * z
    c = c - 0.5 * z + 1.0
    swap = (q & 1) == 1
    cos = jnp.where(swap, s, c)
    sin = jnp.where(swap, c, s)
    cos = jnp.where(((q + 1) & 2) == 2, -cos, cos)
    sin = jnp.where((q & 2) == 2, -sin, sin)
    return cos, sin


def one_hot(count, ids):
    rows = lax.broadcasted_iota(jnp.int32, (count, ids.shape[1]), 0)
    return jnp.where(rows == ids, 1.0, 0.0).astype(BF16)


def mask_of(order, degrees):
    shape = (order.shape[0], degrees)
    n = lax.broadcasted_iota(jnp.int32, shape, 1)
    sine = lax.broadcasted_iota(jnp.int32, shape, 0) & 1
    return (n <= LMAX) & (n >= jnp.maximum(order, 2)) & (order >= sine)


def eight(ref, g):
    return jnp.concatenate([ref[HALF * g + i] for i in range(HALF)], axis=0)


def chunks_of(rows):
    size = 512 if rows % 512 == 0 else rows
    return [(i, size) for i in range(0, rows, size)]


def packed_rows(rows, nodes):
    rest = nodes % LANES
    tall = -(-rows // (LANES // rest) // SUB) * SUB if rest else 0
    return rows * (nodes // LANES) + tall, tall


def pack(x, out_ref, at):
    rows, nodes = x.shape
    rest = nodes % LANES
    for i in range(nodes // LANES):
        out_ref[at + i * rows : at + (i + 1) * rows, :] = x[:, i * LANES : (i + 1) * LANES]
    tall = packed_rows(rows, nodes)[1]
    base = at + rows * (nodes // LANES)
    for i in range(-(-rows // tall) if rest else 0):
        top = min(tall, rows - i * tall)
        out_ref[base : base + top, i * rest : (i + 1) * rest] = x[i * tall : i * tall + top, nodes - rest :]


def unpack(ref, at, rows, nodes):
    rest = nodes % LANES
    parts = [ref[at + i * rows : at + (i + 1) * rows, :] for i in range(nodes // LANES)]
    tall = packed_rows(rows, nodes)[1]
    base = at + rows * (nodes // LANES)
    if rest:
        last = []
        for i in range(-(-rows // tall)):
            top = min(tall, rows - i * tall)
            last.append(ref[base : base + top, i * rest : (i + 1) * rest])
        parts.append(jnp.concatenate(last, axis=0))
    return jnp.concatenate(parts, axis=1)


def order_group(leg, g, x, dims):
    hi, lo = split2(x)
    x2 = jnp.concatenate([hi, lo], axis=0)
    sub = lax.broadcasted_iota(jnp.int32, x2.shape, 0) % SUB // 2
    total = None
    for i in range(HALF):
        term = mm(jnp.where(sub == i, x2, jnp.zeros_like(x2)), leg[g * HALF + i], dims)
        total = term if total is None else total + term
    return total[: x.shape[0]] + total[x.shape[0] :]


def nodal_of(leg, readers, nodal_ref):
    wide = 2 * leg.shape[0]
    for g in range(wide // SUB):
        y = order_group(leg, g, jnp.concatenate([read(g) for read in readers], axis=0), NT)
        for v in range(len(readers)):
            nodal_ref[v * wide + g * SUB : v * wide + (g + 1) * SUB, :] = y[v * SUB : (v + 1) * SUB]


def phase_at(phase_ref, at, size):
    tiles = range(at // LANES, (at + size) // LANES)
    return jnp.concatenate([phase_ref[t] for t in tiles], axis=1)


def rows_of(nodal_ref, phase_ref, data_ref, out_ref, count):
    nodes = nodal_ref.shape[1]
    wide = nodal_ref.shape[0] // count
    hi, lo = split2(nodal_ref[...])
    for at, size in chunks_of(data_ref.shape[1]):
        sel = one_hot(nodes, data_ref[NODE : NODE + 1, at : at + size].astype(jnp.int32))
        terms = mm(hi, sel) + mm(lo, sel)
        ph = phase_at(phase_ref, at, size)
        for v in range(count):
            part = terms[v * wide : (v + 1) * wide] * ph
            out_ref[v : v + 1, at : at + size] = jnp.sum(part, axis=0, keepdims=True)


def gather_nodes(u_list, phase_ref, data_ref, nodes):
    totals = [None] * len(u_list)
    for at, size in chunks_of(data_ref.shape[1]):
        sel = one_hot(nodes, data_ref[NODE : NODE + 1, at : at + size].astype(jnp.int32))
        ph = phase_at(phase_ref, at, size)
        for v, u in enumerate(u_list):
            hi, lo = split2(ph * u[:, at : at + size])
            term = mm(hi, sel, NT) + mm(lo, sel, NT)
            totals[v] = term if totals[v] is None else totals[v] + term
    return totals


def phase_kernel(nodes, slots, data_ref, phase_ref, last_ref, first_ref, order_ref):
    rows = data_ref.shape[1]
    lane = lax.broadcasted_iota(jnp.int32, (2 * slots, slots), 1)
    row = lax.broadcasted_iota(jnp.int32, (2 * slots, slots), 0)
    line = data_ref[ORDER : ORDER + 1, 0:slots]
    twice = jnp.sum(jnp.where(lane == row // 2, line, 0.0), axis=1, keepdims=True)
    order_ref[...] = twice.astype(jnp.int32)
    order = jnp.sum(jnp.where(lane[:slots] == row[:slots], line, 0.0), axis=1, keepdims=True)
    for at, size in chunks_of(rows):
        cos, sin = sincos(data_ref[LON : LON + 1, at : at + size] * order)
        for c, value in enumerate((cos, sin)):
            for t in range(size // LANES):
                tile = value[:, t * LANES : (t + 1) * LANES]
                phase_ref[at // LANES + t, pl.ds(c, slots, stride=2), :] = tile
    seg = data_ref[SEG : SEG + 1, :]
    first = jnp.min(seg, axis=1, keepdims=True)
    last = jnp.max(seg, axis=1, keepdims=True)
    w = data_ref[WEIGHT : WEIGHT + 1, :]
    parts = [jnp.where(seg == last, w, 0.0), jnp.where(seg == first, w, 0.0)]
    totals = gather_nodes(parts, phase_ref, data_ref, nodes)
    for out_ref, total, ident, part in zip((last_ref, first_ref), totals, (last, first), parts):
        pack(total, out_ref, 0)
        amount = jnp.sum(part, axis=1, keepdims=True)
        column = lax.broadcasted_iota(jnp.int32, (SUB, LANES), 1)
        out_ref[out_ref.shape[0] - SUB :, :] = jnp.where(column == 0, amount, ident + 1.0)


def blocks_kernel(pre_hbm, out_ref, pre, sem):
    copy = pltpu.make_async_copy(pre_hbm, pre, sem)
    copy.start()
    copy.wait()

    def one(l, carry):
        for g in range(out_ref.shape[1] // SUB):
            out_ref[l, g * SUB : (g + 1) * SUB, :] = eight(pre.at[l], g)
        return carry

    lax.fori_loop(0, out_ref.shape[0], one, 0)


def forward_kernel(phase_ref, data_ref, order_ref, x_ref, d_ref, leg, out_ref, nodal):
    degrees = x_ref.shape[2]

    def reader(ref):
        def read(g):
            keep = mask_of(order_ref[g * SUB : (g + 1) * SUB, :], degrees)
            return jnp.where(keep, eight(ref, g), 0.0)

        return read

    nodal_of(leg, [reader(x_ref), reader(d_ref)], nodal)
    rows_of(nodal, phase_ref, data_ref, out_ref, 2)


def centered(e_list, weight, seg, prev_row, next_row, segments):
    rows = seg.shape[1]
    ids = lax.broadcasted_iota(jnp.int32, (segments, rows), 0)
    sel = jnp.where(ids == seg, 1.0, 0.0).astype(BF16)
    stack = [weight] + [weight * e for e in e_list]
    pieces = [p for s in stack for p in split3(s)]
    fill = -len(pieces) % 16
    pieces = pieces + [jnp.zeros((fill, rows), BF16)] * (fill > 0)
    sums = mm(jnp.concatenate(pieces, axis=0), sel, NT)
    sums = [sums[3 * i : 3 * i + 1] + sums[3 * i + 1 : 3 * i + 2] + sums[3 * i + 2 : 3 * i + 3] for i in range(len(stack))]
    first = jnp.min(seg, axis=1, keepdims=True)
    last = jnp.max(seg, axis=1, keepdims=True)
    lane = lax.broadcasted_iota(jnp.int32, (1, segments), 1)
    at_first, at_last = lane == first, lane == last
    join_prev = jnp.where(prev_row[:, 1:2] == first.astype(F32) + 1.0, 1.0, 0.0)
    join_next = jnp.where(next_row[:, 1:2] == last.astype(F32) + 1.0, 1.0, 0.0)
    whole = sums[0]
    whole = whole + jnp.where(at_first, join_prev * prev_row[:, 0:1], 0.0)
    whole = whole + jnp.where(at_last, join_next * next_row[:, 0:1], 0.0)
    whole = jnp.where(whole > 0.0, whole, 1.0)
    means = [s / whole for s in sums[1:]]
    pieces = [p for m in means for p in split3(m)]
    fill = -len(pieces) % 16
    pieces = pieces + [jnp.zeros((fill, segments), BF16)]
    spread = mm(jnp.concatenate(pieces, axis=0), sel)
    out = []
    for i, m in enumerate(means):
        mean = spread[3 * i : 3 * i + 1] + spread[3 * i + 1 : 3 * i + 2] + spread[3 * i + 2 : 3 * i + 3]
        to_prev = join_prev * jnp.sum(jnp.where(at_first, m, 0.0), axis=1, keepdims=True)
        to_next = join_next * jnp.sum(jnp.where(at_last, m, 0.0), axis=1, keepdims=True)
        out.append((weight * (e_list[i] - mean), to_prev, to_next))
    return out


def center_and_gather(e_list, data_ref, phase_ref, prev_ref, next_ref, out_ref, segments, nodes):
    wide = phase_ref.shape[1]
    prev_row, next_row = (r[r.shape[0] - SUB : r.shape[0] - SUB + 1, :] for r in (prev_ref, next_ref))
    done = centered(e_list, data_ref[WEIGHT : WEIGHT + 1, :], data_ref[SEG : SEG + 1, :].astype(jnp.int32), prev_row, next_row, segments)
    totals = gather_nodes([u for u, _, _ in done], phase_ref, data_ref, nodes)
    tall = packed_rows(wide, nodes)[0]
    for v, (_, to_prev, to_next) in enumerate(done):
        pack(totals[v], out_ref, v * tall)
        part = slice(v * tall, (v + 1) * tall)
        out_ref[part, :] = out_ref[part, :] - to_prev * prev_ref[0:tall, :] - to_next * next_ref[0:tall, :]


def back_first_kernel(segments, nodes, p_ref, data_ref, phase_ref, prev_ref, next_ref, out_ref):
    e_list = [data_ref[GRAD : GRAD + 1, :] - p_ref[0:1, :], p_ref[1:2, :]]
    center_and_gather(e_list, data_ref, phase_ref, prev_ref, next_ref, out_ref, segments, nodes)


def steps_of(row):
    residual_dot, curvature, first, second = (row[:, i : i + 1] for i in range(4))
    step = residual_dot / curvature
    return step, (first - step * second) / curvature


def back_next_kernel(segments, nodes, p_ref, before_ref, data_ref, phase_ref, prev_ref, next_ref, out_ref):
    rows = data_ref.shape[1]
    step, beta = steps_of(p_ref[0:1, rows : rows + 4])
    e = p_ref[0:1, 0:rows] - step * p_ref[1:2, 0:rows] - beta * before_ref[1:2, :]
    center_and_gather([e], data_ref, phase_ref, prev_ref, next_ref, out_ref, segments, nodes)


def lifted(leg, gathered, store):
    for g in range(gathered[0].shape[0] // SUB):
        x = jnp.concatenate([v[g * SUB : (g + 1) * SUB, :] for v in gathered], axis=0)
        y = order_group(leg, g, x, NN)
        for v in range(len(gathered)):
            store(v, g, y[v * SUB : (v + 1) * SUB])


def precondition(pre, vectors_ref, out_ref):
    degrees = vectors_ref.shape[1]
    wide = pre.shape[1]
    lane = lax.broadcasted_iota(jnp.int32, (1, degrees), 1).astype(F32)
    start_row = (jnp.floor((lane + 0.5) * (1.0 / DB)) * DB).astype(jnp.int32)
    half = degrees // DB // 2 * DB
    base = half // LANES * LANES
    ends = (base + LANES) if half % LANES else half
    ends = min(ends, degrees)
    left = split2(vectors_ref[:, 0:half])
    right = split2(vectors_ref[:, half:])
    near = lax.broadcasted_iota(jnp.int32, (half, ends), 0) - start_row[:, 0:ends]
    far = lax.broadcasted_iota(jnp.int32, (degrees - half, degrees - base), 0) + half - start_row[:, base:]
    for l in range(DB):
        spread = jnp.where(near == l, 1.0, 0.0).astype(BF16)
        a = mm(left[0], spread) + mm(left[1], spread)
        spread = jnp.where(far == l, 1.0, 0.0).astype(BF16)
        b = mm(right[0], spread) + mm(right[1], spread)
        for at in range(0, vectors_ref.shape[0], wide):
            rows = slice(at, at + wide)
            pieces = [
                (slice(0, base), a[rows, 0:base]),
                (slice(base, ends), a[rows, base:ends] + b[rows, 0 : ends - base]),
                (slice(ends, degrees), b[rows, ends - base :]),
            ]
            for lanes, value in pieces:
                if lanes.stop == lanes.start:
                    continue
                term = pre[l, :, lanes] * value
                if l == 0:
                    out_ref[rows, lanes] = term
                else:
                    out_ref[rows, lanes] += term


def scalar_row(values, width):
    lane = lax.broadcasted_iota(jnp.int32, (1, width), 1)
    row = jnp.zeros((1, width), F32)
    for i, value in enumerate(values):
        row = jnp.where(lane == i, value, row)
    return row


def four_dots(pairs):
    sums = [jnp.sum(jnp.sum(a * b, axis=0, keepdims=True), axis=1, keepdims=True) for a, b in pairs]
    return sums


def middle_kernel(
    gathered_ref, phase_ref, data_ref, order_ref, kaula_ref, x_ref, d_ref, leg, pre,
    out_ref, r_ref, q_ref, pr_ref, pq_ref,
    nodal, vec, smooth,
):
    slots, degrees = x_ref.shape[0], x_ref.shape[2]
    nodes = nodal.shape[1]
    wide = 2 * slots
    rows = data_ref.shape[1]
    tall = packed_rows(wide, nodes)[0]

    def store(v, g, y):
        keep = mask_of(order_ref[g * SUB : (g + 1) * SUB, :], degrees)
        k = eight(kaula_ref, g)
        value = y - k * eight(x_ref, g) if v == 0 else y + k * eight(d_ref, g)
        vec[v * wide + g * SUB : v * wide + (g + 1) * SUB, :] = jnp.where(keep, value, 0.0)

    lifted(leg, [unpack(gathered_ref, v * tall, wide, nodes) for v in range(2)], store)
    precondition(pre, vec, smooth)
    keep = mask_of(order_ref[...], degrees)
    r, q = vec[0:wide, :], vec[wide:, :]
    pr = jnp.where(keep, smooth[0:wide, :], 0.0)
    pq = jnp.where(keep, smooth[wide:, :], 0.0)
    d = jnp.where(keep, jnp.concatenate([eight(d_ref, g) for g in range(wide // SUB)], axis=0), 0.0)
    smooth[0:wide, :] = pr
    smooth[wide:, :] = pq
    r_ref[...], q_ref[...], pr_ref[...], pq_ref[...] = r, q, pr, pq
    out_ref[0:1, rows:] = scalar_row(four_dots(((r, d), (d, q), (pr, q), (pq, q))), out_ref.shape[1] - rows)
    out_ref[1:2, rows:] = jnp.zeros((1, out_ref.shape[1] - rows), F32)

    def reader(v):
        return lambda g: smooth[v * wide + g * SUB : v * wide + (g + 1) * SUB, :]

    nodal_of(leg, [reader(0), reader(1)], nodal)
    rows_of(nodal, phase_ref, data_ref, out_ref, 2)


def last_kernel(
    gathered_ref, row_ref, order_ref, kaula_ref, d_ref, r_ref, q_ref, pr_ref, pq_ref, leg, pre,
    dots_ref, q1_ref, pq1_ref,
    d1, smooth,
):
    slots, degrees = d_ref.shape[0], d_ref.shape[2]
    wide = 2 * slots
    at = row_ref.shape[1] - LANES
    step, beta = steps_of(row_ref[0:1, at : at + 4])

    def store(v, g, y):
        part = slice(g * SUB, (g + 1) * SUB)
        keep = mask_of(order_ref[part, :], degrees)
        d = jnp.where(keep, eight(d_ref, g), 0.0)
        new = pr_ref[part, :] - step * pq_ref[part, :] - beta * d
        d1[part, :] = new
        q1_ref[part, :] = jnp.where(keep, y + eight(kaula_ref, g) * new, 0.0)

    nodes = leg.shape[1]
    lifted(leg, [unpack(gathered_ref, 0, wide, nodes)], store)
    precondition(pre, q1_ref, smooth)
    keep = mask_of(order_ref[...], degrees)
    q = q1_ref[...]
    pq = jnp.where(keep, smooth[...], 0.0)
    pq1_ref[...] = pq
    r1 = r_ref[...] - step * q_ref[...]
    pr1 = pr_ref[...] - step * pq_ref[...]
    d = d1[...]
    dots_ref[...] = scalar_row(four_dots(((r1, d), (d, q), (pr1, q), (pq, q))), dots_ref.shape[1])


def final_kernel(
    row_ref, dots_ref, order_ref, x_ref, d_ref, r_ref, q_ref, pr_ref, pq_ref, q1_ref, pq1_ref, ox_ref, or_ref, od_ref
):
    slots, degrees = x_ref.shape[0], x_ref.shape[2]
    at = row_ref.shape[1] - LANES
    step, beta = steps_of(row_ref[0:1, at : at + 4])
    step1, beta1 = steps_of(dots_ref[0:1, 0:4])
    for g in range(2 * slots // SUB):
        part = slice(g * SUB, (g + 1) * SUB)
        keep = mask_of(order_ref[part, :], degrees)
        d = jnp.where(keep, eight(d_ref, g), 0.0)
        pr1 = pr_ref[part, :] - step * pq_ref[part, :]
        d1 = pr1 - beta * d
        x2 = jnp.where(keep, eight(x_ref, g), 0.0) + step * d + step1 * d1
        r2 = r_ref[part, :] - step * q_ref[part, :] - step1 * q1_ref[part, :]
        d2 = pr1 - step1 * pq1_ref[part, :] - beta1 * d1
        for out_ref, value in ((ox_ref, x2), (or_ref, r2), (od_ref, d2)):
            for i in range(HALF):
                out_ref[HALF * g + i] = value[2 * i : 2 * i + 2]


def work(us):
    return pl.CostEstimate(flops=int(us * 1e9), bytes_accessed=int(us * 3e6), transcendentals=0)


def butterfly(x, axis):
    size = lax.axis_size(axis)
    step = 1
    while step < size:
        x = x + lax.ppermute(x, axis, [(i, i ^ step) for i in range(size)])
        step *= 2
    return x


def call(kernel, outs, scratch, n_in, hbm=False, cost=None):
    outs = [o if isinstance(o, jax.ShapeDtypeStruct) else jax.ShapeDtypeStruct(o, F32) for o in outs]
    return pl.pallas_call(
        kernel,
        out_shape=outs,
        in_specs=[HBM if hbm else VMEM] * n_in,
        out_specs=[VMEM for _ in outs],
        scratch_shapes=scratch,
        cost_estimate=cost,
        compiler_params=pltpu.CompilerParams(vmem_limit_bytes=LIMIT),
    )


def shards(longitude, node_index, weight, gradient, segment, order_map, legendre, precond, kaula, start, direction):
    rows = longitude.shape[0]
    slots, nodes, degrees = legendre.shape
    wide = 2 * slots
    tall = packed_rows(wide, nodes)[0]
    segments = lax.axis_size("tm") * lax.axis_size("order")
    kaula, start, direction = (v.transpose(1, 0, 2) for v in (kaula, start, direction))
    pre_all = precond.transpose(0, 2, 1, 3)
    coef = (wide, degrees)
    line = jnp.pad(order_map, (0, rows - slots))
    data = jnp.stack([v.astype(F32) for v in (longitude, node_index, weight, segment, gradient, line)])

    phase, last_edge, first_edge, order = call(
        functools.partial(phase_kernel, nodes, slots),
        [(rows // LANES, wide, LANES)] + [(tall + SUB, LANES)] * 2 + [jax.ShapeDtypeStruct((wide, 1), jnp.int32)],
        [],
        1,
        cost=work(4.0),
    )(data)
    size = lax.axis_size("tm")
    up = [(i, i + 1) for i in range(size - 1)]
    prev_edge = lax.ppermute(last_edge, "tm", up)
    next_edge = lax.ppermute(first_edge, "tm", [(b, a) for a, b in up])
    (pre_all,) = call(
        blocks_kernel,
        [(DB,) + coef],
        [pltpu.VMEM(pre_all.shape, F32), pltpu.SemaphoreType.DMA(())],
        1,
        hbm=True,
        cost=work(3.0),
    )(pre_all)

    (part,) = call(forward_kernel, [(2, rows)], [pltpu.VMEM((2 * wide, nodes), F32)], 6, cost=work(6.0))(
        phase, data, order, start, direction, legendre
    )
    first_rows = butterfly(part, "order")
    (part,) = call(functools.partial(back_first_kernel, segments, nodes), [(2 * tall, LANES)], [], 5, cost=work(2.0))(
        first_rows, data, phase, prev_edge, next_edge
    )
    gathered = butterfly(part, "tm")
    part, r0, q0, pr0, pq0 = call(
        middle_kernel,
        [(2, rows + LANES)] + [coef] * 4,
        [pltpu.VMEM((2 * wide, nodes), F32)] + [pltpu.VMEM((2 * wide, degrees), F32)] * 2,
        9,
        cost=work(10.0),
    )(gathered, phase, data, order, kaula, start, direction, legendre, pre_all)
    next_rows = butterfly(part, "order")
    (part,) = call(functools.partial(back_next_kernel, segments, nodes), [(tall, LANES)], [], 6, cost=work(2.0))(
        next_rows, first_rows, data, phase, prev_edge, next_edge
    )
    gathered = butterfly(part, "tm")
    dots, q1, pq1 = call(last_kernel, [(1, LANES)] + [coef] * 2, [pltpu.VMEM((wide, degrees), F32)] * 2, 11, cost=work(4.0))(
        gathered, next_rows, order, kaula, direction, r0, q0, pr0, pq0, legendre, pre_all
    )
    dots = butterfly(dots, "order")
    outs = call(final_kernel, [(slots, 2, degrees)] * 3, [], 11)(
        next_rows, dots, order, start, direction, r0, q0, pr0, pq0, q1, pq1
    )
    return tuple(o.transpose(1, 0, 2) for o in outs)


def solution(mesh):
    coef = P(None, "order", None)
    placed = (P("tm"),) * 5 + (P("order"), P("order", None, None), P(None, None, "order", None), coef, coef, coef)
    return jax.shard_map(shards, mesh=mesh, in_specs=placed, out_specs=(coef, coef, coef), check_vma=False)
```

```python
import functools

import jax
import jax.numpy as jnp
from jax import lax
from jax.experimental import pallas as pl
from jax.experimental.pallas import tpu as pltpu
from jax.sharding import PartitionSpec as P

LMAX = 300
DB = 19
SUB = 8
HALF = 4
LANES = 128
NODE, WEIGHT, SEG, GRAD, ODD = range(5)
F32 = jnp.float32
BF16 = jnp.bfloat16
NT = (((1,), (1,)), ((), ()))
NN = (((1,), (0,)), ((), ()))
VMEM = pl.BlockSpec(memory_space=pltpu.VMEM)
HBM = pl.BlockSpec(memory_space=pltpu.HBM)
LIMIT = 14 * 1024 * 1024


def mm(a, b, dims=NN):
    return lax.dot_general(a, b, dims, preferred_element_type=F32)


def split2(x):
    hi = x.astype(BF16)
    return hi, (x - hi.astype(F32)).astype(BF16)


def split3(x):
    hi = x.astype(BF16)
    rest = x - hi.astype(F32)
    mid = rest.astype(BF16)
    return hi, mid, (rest - mid.astype(F32)).astype(BF16)


def sincos(angle):
    quadrant = jnp.floor(angle * 0.6366197723675814 + 0.5)
    r = angle - quadrant * 1.5703125
    r = r - quadrant * 4.8351287841796875e-4
    r = r - quadrant * 3.1385570764541626e-7
    r = r - quadrant * 6.077100506506192e-11
    q = quadrant.astype(jnp.int32)
    z = r * r
    s = ((-1.9515295891e-4 * z + 8.3321608736e-3) * z - 1.6666654611e-1) * z * r + r
    c = ((2.443315711809948e-5 * z - 1.388731625493765e-3) * z + 4.166664568298827e-2) * z * z
    c = c - 0.5 * z + 1.0
    swap = (q & 1) == 1
    cos = jnp.where(swap, s, c)
    sin = jnp.where(swap, c, s)
    cos = jnp.where(((q + 1) & 2) == 2, -cos, cos)
    sin = jnp.where((q & 2) == 2, -sin, sin)
    return cos, sin


def one_hot(count, ids):
    rows = lax.broadcasted_iota(jnp.int32, (count, ids.shape[1]), 0)
    return jnp.where(rows == ids, 1.0, 0.0).astype(BF16)


def mask_of(order, degrees):
    shape = (order.shape[0], degrees)
    n = lax.broadcasted_iota(jnp.int32, shape, 1)
    sine = lax.broadcasted_iota(jnp.int32, shape, 0) & 1
    return (n <= LMAX) & (n >= jnp.maximum(order, 2)) & (order >= sine)


def eight(ref, g):
    return jnp.concatenate([ref[HALF * g + i] for i in range(HALF)], axis=0)


def chunks_of(rows):
    size = 512 if rows % 512 == 0 else rows
    return [(i, size) for i in range(0, rows, size)]


def packed_rows(rows, nodes):
    rest = nodes % LANES
    tall = -(-rows // (LANES // rest) // SUB) * SUB if rest else 0
    return rows * (nodes // LANES) + tall, tall


def pack(x, out_ref, at):
    rows, nodes = x.shape
    rest = nodes % LANES
    for i in range(nodes // LANES):
        out_ref[at + i * rows : at + (i + 1) * rows, :] = x[:, i * LANES : (i + 1) * LANES]
    tall = packed_rows(rows, nodes)[1]
    base = at + rows * (nodes // LANES)
    for i in range(-(-rows // tall) if rest else 0):
        top = min(tall, rows - i * tall)
        out_ref[base : base + top, i * rest : (i + 1) * rest] = x[i * tall : i * tall + top, nodes - rest :]


def unpack(ref, at, rows, nodes):
    rest = nodes % LANES
    parts = [ref[at + i * rows : at + (i + 1) * rows, :] for i in range(nodes // LANES)]
    tall = packed_rows(rows, nodes)[1]
    base = at + rows * (nodes // LANES)
    if rest:
        last = []
        for i in range(-(-rows // tall)):
            top = min(tall, rows - i * tall)
            last.append(ref[base : base + top, i * rest : (i + 1) * rest])
        parts.append(jnp.concatenate(last, axis=0))
    return jnp.concatenate(parts, axis=1)


def chunks_at(wide, nodes):
    cut = -(-wide // SUB // 2) * SUB
    out, at = [], 0
    for low, high in ((0, cut), (cut, wide)):
        out.append((low, high - low, at, packed_rows(high - low, nodes)[0]))
        at += out[-1][3]
    return out


def pack_all(x, ref):
    for low, count, at, _ in chunks_at(*x.shape):
        pack(x[low : low + count], ref, at)


def unpack_all(ref, wide, nodes):
    return jnp.concatenate([unpack(ref, at, count, nodes) for _, count, at, _ in chunks_at(wide, nodes)], axis=0)


def group_in(refs, g):
    cut = refs[0].shape[0] // SUB
    at, ref = (g, refs[0]) if g < cut else (g - cut, refs[1])
    return ref[at * SUB : (at + 1) * SUB, :]


def whole_of(refs):
    return jnp.concatenate([ref[...] for ref in refs], axis=0)


def order_group(table, g, x, dims):
    hi, lo = split2(x)
    x2 = jnp.concatenate([hi, lo], axis=0)
    sub = lax.broadcasted_iota(jnp.int32, x2.shape, 0) % SUB // 2
    total = None
    for i in range(HALF):
        term = mm(jnp.where(sub == i, x2, jnp.zeros_like(x2)), table(g * HALF + i), dims)
        total = term if total is None else total + term
    return total[: x.shape[0]] + total[x.shape[0] :]


def nodal_of(table, dims, wide, readers, nodal_ref, start=0):
    for g in range(wide // SUB):
        y = order_group(table, start + g, jnp.concatenate([read(g) for read in readers], axis=0), dims)
        for v in range(len(readers)):
            nodal_ref[v * wide + g * SUB : v * wide + (g + 1) * SUB, :] = y[v * SUB : (v + 1) * SUB]


def phase_at(phase_ref, at, size):
    tiles = range(at // LANES, (at + size) // LANES)
    return jnp.concatenate([phase_ref[t] for t in tiles], axis=1)


def rows_of(nodal, count, phase_ref, data_ref, out_ref):
    nodes = nodal.shape[1]
    wide = nodal.shape[0] // count
    hi, lo = split2(nodal)
    for at, size in chunks_of(data_ref.shape[1]):
        sel = one_hot(nodes, data_ref[NODE : NODE + 1, at : at + size].astype(jnp.int32))
        terms = mm(hi, sel) + mm(lo, sel)
        ph = phase_at(phase_ref, at, size)
        for v in range(count):
            part = terms[v * wide : (v + 1) * wide] * ph
            out_ref[v : v + 1, at : at + size] = jnp.sum(part, axis=0, keepdims=True)


def gather_nodes(u_list, phase_ref, data_ref, nodes):
    totals = [None] * len(u_list)
    for at, size in chunks_of(data_ref.shape[1]):
        sel = one_hot(nodes, data_ref[NODE : NODE + 1, at : at + size].astype(jnp.int32))
        ph = phase_at(phase_ref, at, size)
        for v, u in enumerate(u_list):
            hi, lo = split2(ph * u[:, at : at + size])
            term = mm(hi, sel, NT) + mm(lo, sel, NT)
            totals[v] = term if totals[v] is None else totals[v] + term
    return totals


def block_parts(degrees):
    step = 2 * LANES // (2 * DB) * DB
    spans = [(at, min(at + step, degrees)) for at in range(0, degrees, step)]
    return [(a, b, a // LANES * LANES, min(-(-b // LANES) * LANES, degrees)) for a, b in spans]


def spread_kernel(*refs):
    degrees = sum(ref.shape[1] for ref in refs) // 2
    for ref, (a, b, low, high) in zip(refs, block_parts(degrees)):
        lane = low + lax.broadcasted_iota(jnp.int32, (1, high - low), 1).astype(F32)
        start_row = (jnp.floor((lane + 0.5) * (1.0 / DB)) * DB).astype(jnp.int32)
        row = lax.broadcasted_iota(jnp.int32, (2 * (b - a), high - low), 0)
        source = a + jnp.where(row >= b - a, row - (b - a), row) - start_row
        for l in range(DB):
            ref[l] = jnp.where(source == l, 1.0, 0.0).astype(BF16)


def phase_kernel(
    nodes, odd_ref, line_ref, lon_ref, node_ref, weight_ref, seg_ref, grad_ref, near_ref,
    data_ref, phase_ref, pair_ref, cross_ref, order_ref,
):
    rows = data_ref.shape[1]
    slots = line_ref.shape[1]
    odd = jnp.broadcast_to(odd_ref[0:1, 0:1], (1, 1)) > 0
    for at, ref in ((NODE, node_ref), (WEIGHT, weight_ref), (SEG, seg_ref), (GRAD, grad_ref)):
        data_ref[at : at + 1, :] = ref[...].astype(F32)
    data_ref[ODD : ODD + 1, :] = jnp.broadcast_to(jnp.where(odd, 1.0, 0.0), (1, rows))
    lane = lax.broadcasted_iota(jnp.int32, (2 * slots, slots), 1)
    row = lax.broadcasted_iota(jnp.int32, (2 * slots, slots), 0)
    line = line_ref[...].astype(F32)
    twice = jnp.sum(jnp.where(lane == row // 2, line, 0.0), axis=1, keepdims=True)
    order_ref[...] = twice.astype(jnp.int32)
    order = jnp.sum(jnp.where(lane[:slots] == row[:slots], line, 0.0), axis=1, keepdims=True)
    for at, size in chunks_of(rows):
        cos, sin = sincos(lon_ref[:, at : at + size] * order)
        for c, value in enumerate((cos, sin)):
            for t in range(size // LANES):
                tile = value[:, t * LANES : (t + 1) * LANES]
                phase_ref[at // LANES + t, pl.ds(c, slots, stride=2), :] = tile
    w, at_pair, at_cross = data_ref[WEIGHT : WEIGHT + 1, :], *edge_ids(data_ref)
    idents = (at_pair, at_cross)
    parts = [jnp.where(data_ref[SEG : SEG + 1, :] == ident, w, 0.0) for ident in idents]
    totals = gather_nodes(parts, phase_ref, data_ref, nodes)
    for out_ref, total, ident, part in zip((pair_ref, cross_ref), totals, idents, parts):
        pack_all(total, out_ref)
        amount = jnp.sum(part, axis=1, keepdims=True)
        column = lax.broadcasted_iota(jnp.int32, (SUB, LANES), 1)
        out_ref[out_ref.shape[0] - SUB :, :] = jnp.where(column == 0, amount, ident + 1.0)


def edge_ids(data_ref):
    seg = data_ref[SEG : SEG + 1, :]
    first = jnp.min(seg, axis=1, keepdims=True)
    last = jnp.max(seg, axis=1, keepdims=True)
    odd = data_ref[ODD : ODD + 1, 0:1] > 0
    return jnp.where(odd, first, last), jnp.where(odd, last, first)


def blocks_kernel(pre_hbm, out_ref, pre, sem):
    copy = pltpu.make_async_copy(pre_hbm, pre, sem)
    copy.start()
    copy.wait()

    def one(l, carry):
        for g in range(out_ref.shape[1] // SUB):
            out_ref[l, g * SUB : (g + 1) * SUB, :] = eight(pre.at[l], g)
        return carry

    lax.fori_loop(0, out_ref.shape[0], one, 0)


def forward_kernel(phase_ref, data_ref, order_ref, x_ref, d_ref, leg, out_ref, nodal):
    degrees = x_ref.shape[2]

    def reader(ref):
        def read(g):
            keep = mask_of(order_ref[g * SUB : (g + 1) * SUB, :], degrees)
            return jnp.where(keep, eight(ref, g), 0.0)

        return read

    nodal_of(lambda m: leg[m], NT, 2 * leg.shape[0], [reader(x_ref), reader(d_ref)], nodal)
    rows_of(nodal[...], 2, phase_ref, data_ref, out_ref)


def centered(e_list, weight, seg, idents, rows_beside, segments):
    rows = seg.shape[1]
    ids = lax.broadcasted_iota(jnp.int32, (segments, rows), 0)
    sel = jnp.where(ids == seg, 1.0, 0.0).astype(BF16)
    stack = [weight] + [weight * e for e in e_list]
    pieces = [p for s in stack for p in split3(s)]
    fill = -len(pieces) % 16
    pieces = pieces + [jnp.zeros((fill, rows), BF16)] * (fill > 0)
    sums = mm(jnp.concatenate(pieces, axis=0), sel, NT)
    sums = [sums[3 * i : 3 * i + 1] + sums[3 * i + 1 : 3 * i + 2] + sums[3 * i + 2 : 3 * i + 3] for i in range(len(stack))]
    lane = lax.broadcasted_iota(jnp.int32, (1, segments), 1).astype(F32)
    whole, edges = sums[0], []
    for ident, row in zip(idents, rows_beside):
        join = jnp.where(row[:, 1:2] == ident + 1.0, 1.0, 0.0)
        edges.append((lane == ident, join))
        whole = whole + jnp.where(lane == ident, join * row[:, 0:1], 0.0)
    whole = jnp.where(whole > 0.0, whole, 1.0)
    means = [s / whole for s in sums[1:]]
    pieces = [p for m in means for p in split3(m)]
    fill = -len(pieces) % 16
    pieces = pieces + [jnp.zeros((fill, segments), BF16)]
    spread = mm(jnp.concatenate(pieces, axis=0), sel)
    out = []
    for i, m in enumerate(means):
        mean = spread[3 * i : 3 * i + 1] + spread[3 * i + 1 : 3 * i + 2] + spread[3 * i + 2 : 3 * i + 3]
        beside = [join * jnp.sum(jnp.where(at, m, 0.0), axis=1, keepdims=True) for at, join in edges]
        out.append((weight * (e_list[i] - mean), beside))
    return out


def center_and_gather(e_list, data_ref, phase_ref, pair_ref, cross_ref, out_refs, segments, nodes):
    wide = phase_ref.shape[1]
    chunks = chunks_at(wide, nodes)
    tall = sum(c[3] for c in chunks)
    beside_refs = (pair_ref, cross_ref)
    rows_beside = [r[tall : tall + 1, :] for r in beside_refs]
    weight, seg = data_ref[WEIGHT : WEIGHT + 1, :], data_ref[SEG : SEG + 1, :].astype(jnp.int32)
    done = centered(e_list, weight, seg, edge_ids(data_ref), rows_beside, segments)
    totals = gather_nodes([u for u, _ in done], phase_ref, data_ref, nodes)
    for v, (_, factors) in enumerate(done):
        for i, (low, count, at, high) in enumerate(chunks):
            out_ref, base = (out_refs[0], at) if len(out_refs) == 1 else (out_refs[i], v * high)
            pack(totals[v][low : low + count], out_ref, base)
            part = slice(base, base + high)
            for factor, ref in zip(factors, beside_refs):
                out_ref[part, :] = out_ref[part, :] - factor * ref[at : at + high, :]


def back_first_kernel(segments, nodes, p_ref, data_ref, phase_ref, pair_ref, cross_ref, *out_refs):
    e_list = [data_ref[GRAD : GRAD + 1, :] - p_ref[0:1, :], p_ref[1:2, :]]
    center_and_gather(e_list, data_ref, phase_ref, pair_ref, cross_ref, out_refs, segments, nodes)


def steps_of(row):
    residual_dot, curvature, first, second = (row[:, i : i + 1] for i in range(4))
    step = residual_dot / curvature
    return step, (first - step * second) / curvature


def back_next_kernel(segments, nodes, p_ref, before_ref, data_ref, phase_ref, pair_ref, cross_ref, out_ref):
    rows = data_ref.shape[1]
    step, beta = steps_of(p_ref[0:1, rows : rows + 4])
    e = p_ref[0:1, 0:rows] - step * p_ref[1:2, 0:rows] - beta * before_ref[1:2, :]
    center_and_gather([e], data_ref, phase_ref, pair_ref, cross_ref, [out_ref], segments, nodes)


def lifted(leg, gathered, store, start=0):
    for g in range(gathered[0].shape[0] // SUB):
        x = jnp.concatenate([v[g * SUB : (g + 1) * SUB, :] for v in gathered], axis=0)
        y = order_group(lambda m: leg[m], start + g, x, NN)
        for v in range(len(gathered)):
            store(v, g, y[v * SUB : (v + 1) * SUB])


def precondition(pre, tables, vectors_ref, out_ref, first=0, count=None):
    degrees = vectors_ref.shape[1]
    wide = count or pre.shape[1]
    hi, lo = split2(vectors_ref[...])
    parts = block_parts(degrees)
    pairs = [jnp.concatenate([hi[:, a:b], lo[:, a:b]], axis=1) for a, b, _, _ in parts]
    for l in range(DB):
        each = [mm(pair, table[l]) for pair, table in zip(pairs, tables)]
        for at in range(0, degrees, LANES):
            end = min(at + LANES, degrees)
            value = None
            for term, (_, _, low, high) in zip(each, parts):
                if low <= at and end <= high:
                    term = term[:, at - low : end - low]
                    value = term if value is None else value + term
            for top in range(0, vectors_ref.shape[0], wide):
                term = pre[l, first : first + wide, at:end] * value[top : top + wide]
                if l == 0:
                    out_ref[top : top + wide, at:end] = term
                else:
                    out_ref[top : top + wide, at:end] += term


def scalar_row(values, width):
    lane = lax.broadcasted_iota(jnp.int32, (1, width), 1)
    row = jnp.zeros((1, width), F32)
    for i, value in enumerate(values):
        row = jnp.where(lane == i, value, row)
    return row


def four_dots(pairs):
    sums = [jnp.sum(jnp.sum(a * b, axis=0, keepdims=True), axis=1, keepdims=True) for a, b in pairs]
    return sums


def middle_kernel(start, gathered_ref, order_ref, kaula_ref, x_ref, d_ref, leg, pre, *refs):
    tables, refs = refs[:-8], refs[-8:]
    nodal, dots_ref, r_ref, q_ref, pr_ref, pq_ref, vec, smooth = refs
    degrees = x_ref.shape[2]
    nodes = nodal.shape[1]
    wide = r_ref.shape[0]
    low = start * SUB
    tall = packed_rows(wide, nodes)[0]

    def store(v, g, y):
        keep = mask_of(order_ref[low + g * SUB : low + (g + 1) * SUB, :], degrees)
        k = eight(kaula_ref, start + g)
        value = y - k * eight(x_ref, start + g) if v == 0 else y + k * eight(d_ref, start + g)
        vec[v * wide + g * SUB : v * wide + (g + 1) * SUB, :] = jnp.where(keep, value, 0.0)

    lifted(leg, [unpack(gathered_ref, v * tall, wide, nodes) for v in range(2)], store, start)
    precondition(pre, tables, vec, smooth, low, wide)
    keep = mask_of(order_ref[low : low + wide, :], degrees)
    r, q = vec[0:wide, :], vec[wide:, :]
    pr = jnp.where(keep, smooth[0:wide, :], 0.0)
    pq = jnp.where(keep, smooth[wide:, :], 0.0)
    d = jnp.where(keep, jnp.concatenate([eight(d_ref, start + g) for g in range(wide // SUB)], axis=0), 0.0)
    smooth[0:wide, :] = pr
    smooth[wide:, :] = pq
    r_ref[...], q_ref[...], pr_ref[...], pq_ref[...] = r, q, pr, pq
    dots_ref[...] = scalar_row(four_dots(((r, d), (d, q), (pr, q), (pq, q))), dots_ref.shape[1])

    def reader(v):
        return lambda g: smooth[v * wide + g * SUB : v * wide + (g + 1) * SUB, :]

    nodal_of(lambda m: leg[m], NT, wide, [reader(0), reader(1)], nodal, start)


def middle_rows_kernel(first_ref, second_ref, dots_a, dots_b, phase_ref, data_ref, out_ref):
    rows = data_ref.shape[1]
    parts = []
    for v in range(2):
        for ref in (first_ref, second_ref):
            half = ref.shape[0] // 2
            parts.append(ref[v * half : (v + 1) * half, :])
    out_ref[0:1, rows:] = dots_a[...] + dots_b[...]
    out_ref[1:2, rows:] = jnp.zeros((1, out_ref.shape[1] - rows), F32)
    rows_of(jnp.concatenate(parts, axis=0), 2, phase_ref, data_ref, out_ref)


def last_kernel(gathered_ref, row_ref, order_ref, kaula_ref, d_ref, *refs):
    r_refs, q_refs, pr_refs, pq_refs = (refs[i : i + 2] for i in range(0, 8, 2))
    leg, pre, tables, refs = refs[8], refs[9], refs[10:-5], refs[-5:]
    dots_ref, q1_ref, pq1_ref, d1, smooth = refs
    slots, degrees = d_ref.shape[0], d_ref.shape[2]
    wide = 2 * slots
    at = row_ref.shape[1] - LANES
    step, beta = steps_of(row_ref[0:1, at : at + 4])

    def store(v, g, y):
        part = slice(g * SUB, (g + 1) * SUB)
        keep = mask_of(order_ref[part, :], degrees)
        d = jnp.where(keep, eight(d_ref, g), 0.0)
        new = group_in(pr_refs, g) - step * group_in(pq_refs, g) - beta * d
        d1[part, :] = new
        q1_ref[part, :] = jnp.where(keep, y + eight(kaula_ref, g) * new, 0.0)

    nodes = leg.shape[1]
    lifted(leg, [unpack_all(gathered_ref, wide, nodes)], store)
    precondition(pre, tables, q1_ref, smooth)
    keep = mask_of(order_ref[...], degrees)
    q = q1_ref[...]
    pq = jnp.where(keep, smooth[...], 0.0)
    pq1_ref[...] = pq
    r1 = whole_of(r_refs) - step * whole_of(q_refs)
    pr1 = whole_of(pr_refs) - step * whole_of(pq_refs)
    d = d1[...]
    dots_ref[...] = scalar_row(four_dots(((r1, d), (d, q), (pr1, q), (pq, q))), dots_ref.shape[1])


def final_kernel(row_ref, dots_ref, order_ref, x_ref, d_ref, *refs):
    r_refs, q_refs, pr_refs, pq_refs = (refs[i : i + 2] for i in range(0, 8, 2))
    q1_ref, pq1_ref, ox_ref, or_ref, od_ref = refs[8:]
    slots, degrees = x_ref.shape[0], x_ref.shape[2]
    at = row_ref.shape[1] - LANES
    step, beta = steps_of(row_ref[0:1, at : at + 4])
    step1, beta1 = steps_of(dots_ref[0:1, 0:4])
    for g in range(2 * slots // SUB):
        part = slice(g * SUB, (g + 1) * SUB)
        keep = mask_of(order_ref[part, :], degrees)
        d = jnp.where(keep, eight(d_ref, g), 0.0)
        pr1 = group_in(pr_refs, g) - step * group_in(pq_refs, g)
        d1 = pr1 - beta * d
        x2 = jnp.where(keep, eight(x_ref, g), 0.0) + step * d + step1 * d1
        r2 = group_in(r_refs, g) - step * group_in(q_refs, g) - step1 * q1_ref[part, :]
        d2 = pr1 - step1 * pq1_ref[part, :] - beta1 * d1
        for out_ref, value in ((ox_ref, x2), (or_ref, r2), (od_ref, d2)):
            for i in range(HALF):
                out_ref[HALF * g + i] = value[2 * i : 2 * i + 2]


def work(us):
    return pl.CostEstimate(flops=int(us * 1e9), bytes_accessed=int(us * 3e6), transcendentals=0)


def steps_over(axis):
    size = lax.axis_size(axis)
    return [1 << i for i in range(size.bit_length() - 1)]


def exchanged(x, axis, step):
    return x + lax.ppermute(x, axis, [(i, i ^ step) for i in range(lax.axis_size(axis))])


def butterfly(x, axis):
    for step in steps_over(axis):
        x = exchanged(x, axis, step)
    return x


def butterflies(first, second, axis):
    steps = steps_over(axis)
    for a, b in zip(steps, steps[1:] + steps[:1]):
        first, second = exchanged(first, axis, a), exchanged(second, axis, b)
    return first, second


def call(kernel, outs, scratch, n_in, hbm=False, cost=None):
    outs = [o if isinstance(o, jax.ShapeDtypeStruct) else jax.ShapeDtypeStruct(o, F32) for o in outs]
    return pl.pallas_call(
        kernel,
        out_shape=outs,
        in_specs=[HBM if hbm else VMEM] * n_in,
        out_specs=[VMEM for _ in outs],
        scratch_shapes=scratch,
        cost_estimate=cost,
        compiler_params=pltpu.CompilerParams(vmem_limit_bytes=LIMIT),
    )


def shards(longitude, node_index, weight, gradient, segment, order_map, legendre, precond, kaula, start, direction):
    rows = longitude.shape[0]
    slots, nodes, degrees = legendre.shape
    wide = 2 * slots
    chunks = chunks_at(wide, nodes)
    tall = sum(c[3] for c in chunks)
    segments = lax.axis_size("tm") * lax.axis_size("order")
    kaula, start, direction = (v.transpose(1, 0, 2) for v in (kaula, start, direction))
    pre_all = precond.transpose(0, 2, 1, 3)
    coef = (wide, degrees)
    shapes = [(DB, 2 * (b - a), high - low) for a, b, low, high in block_parts(degrees)]
    tables = call(spread_kernel, [jax.ShapeDtypeStruct(t, BF16) for t in shapes], [], 0, cost=work(4.0))()
    odd = (lax.axis_index("tm") % 2).reshape(1, 1)
    line = [v.reshape(1, -1) for v in (order_map, longitude, node_index, weight, segment, gradient)]
    data, phase, pair_edge, cross_edge, order = call(
        functools.partial(phase_kernel, nodes),
        [(SUB, rows), (rows // LANES, wide, LANES)] + [(tall + SUB, LANES)] * 2 + [jax.ShapeDtypeStruct((wide, 1), jnp.int32)],
        [],
        8,
        cost=work(4.0),
    )(odd, *line, tables[0])
    size = lax.axis_size("tm")
    pair_edge = lax.ppermute(pair_edge, "tm", [(i, i ^ 1) for i in range(size)])
    cross = [(i, i + 1) for i in range(1, size - 1, 2)]
    cross_edge = lax.ppermute(cross_edge, "tm", cross + [(b, a) for a, b in cross])
    (pre_all,) = call(
        blocks_kernel,
        [(DB,) + coef],
        [pltpu.VMEM(pre_all.shape, F32), pltpu.SemaphoreType.DMA(())],
        1,
        hbm=True,
        cost=work(3.0),
    )(pre_all)

    (part,) = call(forward_kernel, [(2, rows)], [pltpu.VMEM((2 * wide, nodes), F32)], 6, cost=work(6.0))(
        phase, data, order, start, direction, legendre
    )
    first_rows = butterfly(part, "order")
    first_rows, pre_all = lax.optimization_barrier((first_rows, pre_all))
    parts = call(
        functools.partial(back_first_kernel, segments, nodes), [(2 * c[3], LANES) for c in chunks], [], 5, cost=work(2.0)
    )(first_rows, data, phase, pair_edge, cross_edge)
    middle = [
        call(
            functools.partial(middle_kernel, low // SUB),
            [(2 * count, nodes), (1, LANES)] + [(count, degrees)] * 4,
            [pltpu.VMEM((2 * count, degrees), F32)] * 2,
            7 + len(tables),
            cost=work(4.0),
        )(gathered, order, kaula, start, direction, legendre, pre_all, *tables)
        for (low, count, _, _), gathered in zip(chunks, butterflies(*parts, "tm"))
    ]
    (nodal_a, dots_a, *halves_a), (nodal_b, dots_b, *halves_b) = middle
    state = [v for pair in zip(halves_a, halves_b) for v in pair]
    (part,) = call(middle_rows_kernel, [(2, rows + LANES)], [], 6, cost=work(2.0))(
        nodal_a, nodal_b, dots_a, dots_b, phase, data
    )
    next_rows = butterfly(part, "order")
    (part,) = call(functools.partial(back_next_kernel, segments, nodes), [(tall, LANES)], [], 6, cost=work(2.0))(
        next_rows, first_rows, data, phase, pair_edge, cross_edge
    )
    gathered = butterfly(part, "tm")
    dots, q1, pq1 = call(last_kernel, [(1, LANES)] + [coef] * 2, [pltpu.VMEM((wide, degrees), F32)] * 2, 15 + len(tables), cost=work(4.0))(
        gathered, next_rows, order, kaula, direction, *state, legendre, pre_all, *tables
    )
    dots = butterfly(dots, "order")
    outs = call(final_kernel, [(slots, 2, degrees)] * 3, [], 15)(
        next_rows, dots, order, start, direction, *state, q1, pq1
    )
    return tuple(o.transpose(1, 0, 2) for o in outs)


def solution(mesh):
    coef = P(None, "order", None)
    placed = (P("tm"),) * 5 + (P("order"), P("order", None, None), P(None, None, "order", None), coef, coef, coef)
    return jax.shard_map(shards, mesh=mesh, in_specs=placed, out_specs=(coef, coef, coef), check_vma=False)
```
